32 devices in a mesh: groups: 2 (over y), blk: 8 (over z, x), uly: 2 (over core).
Axes of the slice: x: 2, y: 2, z: 4, core: 2. Of those that a mesh axis runs over, the one named last changes fastest.
Arguments:
- query_proj: bfloat16 [4096, 4096], P(('groups', 'blk', 'uly')), parts along dimension 0, may hold values from -17 to 17
- key_proj: bfloat16 [4096, 512], P(('groups', 'blk', 'uly')), parts along dimension 0, may hold values from -17 to 17
- value_projection: bfloat16 [4096, 512], P(('groups', 'blk', 'uly')), parts along dimension 0, may hold values from -6 to 6
- query_gain: float32 [128], replicated, may hold values from 0.5 to 6
- key_gain: float32 [128], replicated, may hold values from 0.5 to 6
Outputs:
- attended: bfloat16 [4096, 4096], P(('groups', 'blk', 'uly')), parts along dimension 0
The draws below stay inside these ranges and needn't reach their ends.
There are 2 independent parts, one for each index of `groups`. The reference program is written for one: setup_inputs(seed, part) draws one part's arguments, and reference() takes and returns one part's arrays. A program takes and returns all parts, laid end to end along the dimension named above; an argument that names none is the same for every part. Nothing has to cross between parts.
All inputs are finite; a program needn't handle non-finite values.
Results may differ from the reference program's by a relative error of at most 0.0085.
The reference program's roundings to bfloat16 on the way count: a program that leaves them out, or rounds other values in their place, can miss the bound.
Values may be sent and summed in bfloat16 or wider, within the bound.
A program may use at most 64 MiB of HBM per device.

```python
import math
import jax
import jax.numpy as jnp
from jax import lax

STRETCH_TOKENS = 128
QUERY_HEADS = 32
KEY_VALUE_HEADS = 4
HEAD_SIZE = 128
WINDOW_TOKENS = 128
SEQUENCE_TOKENS = 2048
N_BLK = 8


def flagged_rows(key, row_count, head_count):
    sample = jnp.clip(jax.random.normal(key, (row_count, head_count, HEAD_SIZE), jnp.float32), -6.0, 6.0)
    return sample.reshape(row_count, head_count * HEAD_SIZE)


def gain_table(key, salt):
    own_key = jax.random.fold_in(key, salt)
    scales = jnp.exp(jax.random.uniform(own_key, (HEAD_SIZE,), jnp.float32, math.log(0.5), math.log(2.0)))
    return scales


def draw_query_proj(key, part):
    return flagged_rows(key, SEQUENCE_TOKENS, QUERY_HEADS).astype(jnp.bfloat16)


def draw_key_proj(key, part):
    return flagged_rows(key, SEQUENCE_TOKENS, KEY_VALUE_HEADS).astype(jnp.bfloat16)


def draw_query_gain(key, part):
    return gain_table(key, 101)


def draw_key_gain(key, part):
    return gain_table(key, 202)


def steps_of(stream_key, extent, cuts, least, largest):
    gain, own = 1.0, jax.random.fold_in(stream_key, 6)
    for dim, blocks in cuts:
        draws = jnp.exp(jax.random.uniform(jax.random.fold_in(own, dim), (blocks,), jnp.float32, least / len(cuts), largest / len(cuts)))
        gain = gain * jnp.repeat(draws, extent[dim] // blocks).reshape([-1 if axis == dim else 1 for axis in range(len(extent))])
    return gain


def normal_values(key, shape, width, bound, cuts=(), kind=jnp.bfloat16):
    array = jax.random.normal(key, shape, jnp.float32) * width
    if len(cuts) > 0:
        array = steps_of(key, shape, cuts, -0.22, 0.18) * array
    return jnp.clip(array, min=-bound, max=bound).astype(kind)


def setup_inputs(seed: int = 0, part: int = 0) -> dict:
    key_list = jax.random.split(jax.random.key(seed), 6)
    part_splits = jax.random.split(jax.random.fold_in(key_list[5], part), 6)
    return {
        "query_proj": draw_query_proj(jax.random.fold_in(jax.random.fold_in(key_list[5], part), 71), part),
        "key_proj": draw_key_proj(jax.random.fold_in(jax.random.fold_in(key_list[5], part), 71), part),
        "value_projection": normal_values(part_splits[2], (SEQUENCE_TOKENS, KEY_VALUE_HEADS * HEAD_SIZE), 1.0, 6.0, ((0, 16),)),
        "query_gain": draw_query_gain(jax.random.fold_in(key_list[5], 71), part),
        "key_gain": draw_key_gain(jax.random.fold_in(key_list[5], 71), part),
    }


NEG_FILL = -1e+30
ROPE_BASE = 1000000.0

def rotate_rows(source, scales, positions):
    head_width = scales.shape[0]
    row_count = source.shape[0]
    head_count = source.shape[1] // head_width
    values = source.astype(jnp.float32).reshape(row_count, head_count, head_width)
    mean_square = lax.optimization_barrier(jnp.mean(values * values, axis=-1, keepdims=True))
    normed = values * lax.rsqrt(mean_square + 1e-06) * scales.astype(jnp.float32)
    half_width = head_width // 2
    frequency = jnp.exp(jnp.arange(half_width, dtype=jnp.float32) * (-2.0 * math.log(ROPE_BASE) / head_width))
    angles = positions.astype(jnp.float32)[:, None] * frequency[None, :]
    cosine = jnp.cos(angles)[:, None, :]
    sine = jnp.sin(angles)[:, None, :]
    first_half = normed[..., :half_width]
    second_half = normed[..., half_width:]
    rotated = jnp.concatenate([first_half * cosine - second_half * sine, second_half * cosine + first_half * sine], axis=-1)
    return rotated.reshape(row_count, head_count * head_width).astype(jnp.bfloat16)

def reference(query_proj, key_proj, value_projection, query_gain, key_gain):
    seq_len = SEQUENCE_TOKENS
    stored = jnp.arange(seq_len, dtype=jnp.int32)
    stored_block = stored // STRETCH_TOKENS
    cycle_pos = stored_block // 2
    stretch_id = jnp.where(stored_block % 2 == 0, cycle_pos, 2 * N_BLK - 1 - cycle_pos)
    position = (stretch_id * STRETCH_TOKENS + stored % STRETCH_TOKENS).astype(jnp.int32)
    query_rot = rotate_rows(query_proj, query_gain, position)
    key_rot = rotate_rows(key_proj, key_gain, position)
    natural = jnp.arange(seq_len, dtype=jnp.int32)
    natural_stretch = natural // STRETCH_TOKENS
    stored_slot = jnp.where(natural_stretch < N_BLK, 2 * natural_stretch, 2 * (2 * N_BLK - 1 - natural_stretch) + 1)
    source = (stored_slot * STRETCH_TOKENS + natural % STRETCH_TOKENS).astype(jnp.int32)
    query_sequence = query_rot[source]
    key_sequence = key_rot[source]
    value_sequence = value_projection[source]
    key_padded = jnp.concatenate([jnp.zeros((WINDOW_TOKENS, KEY_VALUE_HEADS * HEAD_SIZE), jnp.bfloat16), key_sequence], axis=0)
    value_padded = jnp.concatenate([jnp.zeros((WINDOW_TOKENS, KEY_VALUE_HEADS * HEAD_SIZE), jnp.bfloat16), value_sequence], axis=0)
    group_count = QUERY_HEADS // KEY_VALUE_HEADS

    def one_stretch(stretch_index):
        starting_row = (stretch_index * STRETCH_TOKENS).astype(jnp.int32)
        query_tile = lax.dynamic_slice_in_dim(query_sequence, starting_row, STRETCH_TOKENS, 0).astype(jnp.float32).reshape(STRETCH_TOKENS, KEY_VALUE_HEADS, group_count, HEAD_SIZE)
        key_tile = lax.dynamic_slice_in_dim(key_padded, starting_row, WINDOW_TOKENS + STRETCH_TOKENS, 0).astype(jnp.float32).reshape(WINDOW_TOKENS + STRETCH_TOKENS, KEY_VALUE_HEADS, HEAD_SIZE)
        value_tile = lax.dynamic_slice_in_dim(value_padded, starting_row, WINDOW_TOKENS + STRETCH_TOKENS, 0).astype(jnp.float32).reshape(WINDOW_TOKENS + STRETCH_TOKENS, KEY_VALUE_HEADS, HEAD_SIZE)
        scores = jnp.einsum('rkgd,nkd->kgrn', query_tile, key_tile) * (1.0 / math.sqrt(HEAD_SIZE))
        query_pos = starting_row + jnp.arange(STRETCH_TOKENS, dtype=jnp.int32)
        key_pos = starting_row - WINDOW_TOKENS + jnp.arange(WINDOW_TOKENS + STRETCH_TOKENS, dtype=jnp.int32)
        distance = query_pos[:, None] - key_pos[None, :]
        allowed = (distance >= 0) & (distance < WINDOW_TOKENS) & (key_pos >= 0)[None, :]
        scores = jnp.where(allowed, scores, NEG_FILL)
        top_score = lax.optimization_barrier(jnp.max(scores, axis=-1, keepdims=True))
        weights = jnp.exp(scores - top_score)
        total_weight = lax.optimization_barrier(jnp.sum(weights, axis=-1))
        rounded = lax.optimization_barrier(weights.astype(jnp.bfloat16)).astype(jnp.float32)
        mixed_rows = jnp.einsum('kgrn,nkd->kgrd', rounded, value_tile) / total_weight[..., None]
        return jnp.transpose(mixed_rows, (2, 0, 1, 3)).reshape(STRETCH_TOKENS, QUERY_HEADS * HEAD_SIZE).astype(jnp.bfloat16)
    stretches = lax.map(one_stretch, jnp.arange(2 * N_BLK, dtype=jnp.int32))
    out_seq = stretches.reshape(seq_len, QUERY_HEADS * HEAD_SIZE)
    return out_seq[position]
```

```python
import functools
import math

import jax
import jax.numpy as jnp
from jax import lax
from jax.experimental import pallas as pl
from jax.experimental.pallas import tpu as pltpu
from jax.sharding import PartitionSpec as P

NEG_FILL = -1e30
ROPE_BASE = 1000000.0
EPS = 1e-06
MESH = pl.DeviceIdType.MESH


def rope_tables(first_pos, rows, frequency, sign, gain, gain_swapped):
    eight = lax.broadcasted_iota(jnp.int32, (8, 128), 0).astype(jnp.float32)
    fine = eight * frequency
    fine_cos, fine_sin = jnp.cos(fine), jnp.sin(fine)
    steps = rows // 8
    coarse_pos = first_pos + 8 * lax.broadcasted_iota(jnp.int32, (steps, 128), 0)
    coarse = coarse_pos.astype(jnp.float32) * frequency
    coarse_cos, coarse_sin = jnp.cos(coarse), jnp.sin(coarse)
    cosines, sines = [], []
    for j in range(steps):
        cos_j, sin_j = coarse_cos[j : j + 1], coarse_sin[j : j + 1]
        cosines.append((cos_j * fine_cos - sin_j * fine_sin) * gain)
        sines.append((sin_j * fine_cos + cos_j * fine_sin) * (sign * gain_swapped))
    return jnp.concatenate(cosines), jnp.concatenate(sines)


def rotate(x, table_a, table_b):
    x = x.astype(jnp.float32)
    r = lax.rsqrt(jnp.mean(x * x, axis=-1, keepdims=True) + EPS)
    swapped = pltpu.roll(x, x.shape[1] // 2, 1)
    return ((x * table_a + swapped * table_b) * r).astype(jnp.bfloat16)


def kernel(
    cycle, span, kv_heads, group,
    q_hbm, k_hbm, v_hbm, qg_hbm, kg_hbm, o_ref,
    q_buf, kv_own, kv_prev, q_rot, k_cat, v_cat, tab, gains,
    q_sem, own_sem, gain_sem, send_sem, recv_sem,
):
    rows, head = k_hbm.shape[0], qg_hbm.shape[1]
    width = group * head
    blk, uly = lax.axis_index("blk"), lax.axis_index("uly")
    last = 2 * cycle - 1
    stretch = jnp.where(uly == 0, blk, last - blk)

    def device_of(index):
        low = index < cycle
        return {"blk": jnp.where(low, index, last - index), "uly": jnp.where(low, 0, 1)}

    barrier = pltpu.get_barrier_semaphore()
    for d in range(1, span + 1):

        @pl.when(stretch >= d)
        def _(d=d):
            pl.semaphore_signal(
                barrier, inc=1, device_id=device_of(stretch - d), device_id_type=MESH
            )

    own_copies = [
        pltpu.make_async_copy(src, kv_own.at[i], own_sem.at[i])
        for i, src in enumerate((k_hbm, v_hbm))
    ]
    q_copies = [
        pltpu.make_async_copy(
            q_hbm.at[:, pl.ds(h * width, width)], q_buf.at[h], q_sem.at[h]
        )
        for h in range(kv_heads)
    ]

    gain_copies = [
        pltpu.make_async_copy(src, gains.at[i], gain_sem.at[i])
        for i, src in enumerate((qg_hbm, kg_hbm))
    ]

    def remote(d, h, i):
        src = (k_hbm, v_hbm)[i]
        return pltpu.make_async_remote_copy(
            src_ref=src.at[:, pl.ds(h * head, head)],
            dst_ref=kv_prev.at[d - 1, i, h],
            send_sem=send_sem.at[d - 1, i, h],
            recv_sem=recv_sem.at[d - 1, i, h],
            device_id=device_of(stretch + d),
            device_id_type=MESH,
        )

    for copy in gain_copies + own_copies[:1] + q_copies + own_copies[1:]:
        copy.start()

    for d in range(1, span + 1):

        @pl.when(stretch + d <= last)
        def _():
            pl.semaphore_wait(barrier, 1)

    for h in range(kv_heads):
        for i in range(2):
            for d in range(1, span + 1):

                @pl.when(stretch + d <= last)
                def _(d=d, h=h, i=i):
                    remote(d, h, i).start()

    for d in range(1, span + 1):

        @pl.when(stretch < d)
        def _(d=d):
            kv_prev[d - 1] = jnp.zeros_like(kv_prev[d - 1])

    half = head // 2
    lane = lax.broadcasted_iota(jnp.int32, (1, head), 1)
    frequency = jnp.exp(
        lax.rem(lane, half).astype(jnp.float32) * (-2.0 * math.log(ROPE_BASE) / head)
    )
    sign = jnp.where(lane < half, -1.0, 1.0)
    for copy in gain_copies:
        copy.wait()
    q_gain, k_gain = gains[0], gains[1]
    q_swap, k_swap = pltpu.roll(q_gain, half, 1), pltpu.roll(k_gain, half, 1)
    tables = functools.partial(rope_tables, rows=rows, frequency=frequency, sign=sign)
    tab[0, 0], tab[0, 1] = tables(stretch * rows, gain=q_gain, gain_swapped=q_swap)
    for d in range(span + 1):
        tab[d + 1, 0], tab[d + 1, 1] = tables(
            (stretch - d) * rows, gain=k_gain, gain_swapped=k_swap
        )

    own_copies[0].wait()
    for h in range(kv_heads):
        k_cat[h, :rows] = rotate(
            kv_own[0, :, h * head : (h + 1) * head], tab[1, 0], tab[1, 1]
        )
    for h in range(kv_heads):
        q_copies[h].wait()
        for g in range(group):
            q_rot[h, g * rows : (g + 1) * rows] = rotate(
                q_buf[h, :, g * head : (g + 1) * head], tab[0, 0], tab[0, 1]
            )
    own_copies[1].wait()
    for h in range(kv_heads):
        v_cat[h, :rows] = kv_own[1, :, h * head : (h + 1) * head]

    row = lax.broadcasted_iota(jnp.int32, (rows, rows), 0)
    col = lax.broadcasted_iota(jnp.int32, (rows, rows), 1)
    own = col <= row
    scale = 1.0 / math.sqrt(head)
    bias = [
        jnp.where(stretch >= d, 0.0, NEG_FILL).astype(jnp.float32)
        for d in range(1, span + 1)
    ]

    for h in range(kv_heads):
        for d in range(1, span + 1):

            @pl.when(stretch >= d)
            def _(d=d, h=h):
                remote(d, h, 0).wait_recv()

            k_cat[h, d * rows : (d + 1) * rows] = rotate(
                kv_prev[d - 1, 0, h], tab[d + 1, 0], tab[d + 1, 1]
            )

            @pl.when(stretch >= d)
            def _(d=d, h=h):
                remote(d, h, 1).wait_recv()

            v_cat[h, d * rows : (d + 1) * rows] = kv_prev[d - 1, 1, h]

        keys, values = k_cat[h], v_cat[h]
        for g in range(group):
            scores = lax.dot_general(
                q_rot[h, g * rows : (g + 1) * rows],
                keys,
                (((1,), (1,)), ((), ())),
                preferred_element_type=jnp.float32,
            )
            parts = [scores[:, d * rows : (d + 1) * rows] for d in range(span + 1)]
            tiles = [jnp.where(own, parts[0], parts[span] + bias[span - 1])]
            tiles += [parts[d] + bias[d - 1] for d in range(1, span)]
            top = functools.reduce(jnp.maximum, tiles)
            top = jnp.max(top, axis=-1, keepdims=True)
            weights = [jnp.exp((tile - top) * scale) for tile in tiles]
            total = jnp.sum(functools.reduce(jnp.add, weights), axis=-1, keepdims=True)
            near = jnp.where(own, weights[0], 0.0)
            far = jnp.where(own, 0.0, weights[0])
            rounded = jnp.concatenate([near] + weights[1:] + [far], axis=1)
            mixed = jnp.dot(
                rounded.astype(jnp.bfloat16), values, preferred_element_type=jnp.float32
            )
            o_ref[:, h * width + g * head : h * width + (g + 1) * head] = (
                mixed / total
            ).astype(o_ref.dtype)

    for h in range(kv_heads):
        for i in range(2):
            for d in range(1, span + 1):

                @pl.when(stretch + d <= last)
                def _(d=d, h=h, i=i):
                    remote(d, h, i).wait_send()


def local(query_proj, key_proj, value_projection, query_gain, key_gain):
    cycle = lax.axis_size("blk")
    span = max(1, cycle // 64)
    rows, head = query_proj.shape[0], query_gain.shape[0]
    kv_heads = key_proj.shape[1] // head
    group = query_proj.shape[1] // head // kv_heads
    bf16 = jnp.bfloat16
    vmem = pl.BlockSpec(memory_space=pltpu.VMEM)
    hbm = pl.BlockSpec(memory_space=pltpu.HBM)
    return pl.pallas_call(
        functools.partial(kernel, cycle, span, kv_heads, group),
        out_shape=jax.ShapeDtypeStruct(query_proj.shape, bf16),
        in_specs=[hbm] * 5,
        out_specs=vmem,
        scratch_shapes=[
            pltpu.VMEM((kv_heads, rows, group * head), bf16),
            pltpu.VMEM((2, rows, kv_heads * head), bf16),
            pltpu.VMEM((span, 2, kv_heads, rows, head), bf16),
            pltpu.VMEM((kv_heads, group * rows, head), bf16),
            pltpu.VMEM((kv_heads, (span + 1) * rows, head), bf16),
            pltpu.VMEM((kv_heads, (span + 1) * rows, head), bf16),
            pltpu.VMEM((span + 2, 2, rows, head), jnp.float32),
            pltpu.VMEM((2, 1, head), jnp.float32),
            pltpu.SemaphoreType.DMA((kv_heads,)),
            pltpu.SemaphoreType.DMA((2,)),
            pltpu.SemaphoreType.DMA((2,)),
            pltpu.SemaphoreType.DMA((span, 2, kv_heads)),
            pltpu.SemaphoreType.DMA((span, 2, kv_heads)),
        ],
        compiler_params=pltpu.CompilerParams(
            collective_id=0, has_side_effects=True, vmem_limit_bytes=16 * 1024 * 1024
        ),
        name="window_attention",
    )(
        query_proj,
        key_proj,
        value_projection,
        query_gain.reshape(1, head),
        key_gain.reshape(1, head),
    )


def solution(mesh):
    rows = P(("groups", "blk", "uly"), None)
    return jax.shard_map(
        local,
        mesh=mesh,
        in_specs=(rows, rows, rows, P(), P()),
        out_specs=rows,
        check_vma=False,
    )
```

```python
import functools
import math

import jax
import jax.numpy as jnp
from jax import lax
from jax.experimental import pallas as pl
from jax.experimental.pallas import tpu as pltpu
from jax.sharding import PartitionSpec as P

NEG_FILL = -1e30
ROPE_BASE = 1000000.0
EPS = 1e-06
MESH = pl.DeviceIdType.MESH


def rope_tables(first_pos, rows, frequency, sign, gain, gain_swapped):
    eight = lax.broadcasted_iota(jnp.int32, (8, 128), 0).astype(jnp.float32)
    fine = eight * frequency
    fine_cos, fine_sin = jnp.cos(fine), jnp.sin(fine)
    steps = rows // 8
    coarse_pos = first_pos + 8 * lax.broadcasted_iota(jnp.int32, (steps, 128), 0)
    coarse = coarse_pos.astype(jnp.float32) * frequency
    coarse_cos, coarse_sin = jnp.cos(coarse), jnp.sin(coarse)
    cosines, sines = [], []
    for j in range(steps):
        cos_j, sin_j = coarse_cos[j : j + 1], coarse_sin[j : j + 1]
        cosines.append((cos_j * fine_cos - sin_j * fine_sin) * gain)
        sines.append((sin_j * fine_cos + cos_j * fine_sin) * (sign * gain_swapped))
    return jnp.concatenate(cosines), jnp.concatenate(sines)


def rotate(x, table_a, table_b):
    x = x.astype(jnp.float32)
    r = lax.rsqrt(jnp.mean(x * x, axis=-1, keepdims=True) + EPS)
    swapped = pltpu.roll(x, x.shape[1] // 2, 1)
    return ((x * table_a + swapped * table_b) * r).astype(jnp.bfloat16)


def kernel(
    cycle, span, kv_heads, group,
    q_hbm, k_hbm, v_hbm, qg_hbm, kg_hbm, o_ref,
    q_buf, kv_own, kv_prev, q_rot, k_cat, v_cat, tab, gains,
    q_sem, own_sem, gain_sem, send_sem, recv_sem,
):
    rows, head = k_hbm.shape[0], qg_hbm.shape[1]
    width = group * head
    blk, uly = lax.axis_index("blk"), lax.axis_index("uly")
    last = 2 * cycle - 1
    stretch = jnp.where(uly == 0, blk, last - blk)

    def device_of(index):
        low = index < cycle
        return {"blk": jnp.where(low, index, last - index), "uly": jnp.where(low, 0, 1)}

    barrier = pltpu.get_barrier_semaphore()
    for d in range(1, span + 1):

        @pl.when(stretch >= d)
        def _(d=d):
            pl.semaphore_signal(
                barrier, inc=1, device_id=device_of(stretch - d), device_id_type=MESH
            )

    own_copies = [
        pltpu.make_async_copy(src, kv_own.at[i], own_sem.at[i])
        for i, src in enumerate((k_hbm, v_hbm))
    ]
    q_copies = [
        pltpu.make_async_copy(
            q_hbm.at[:, pl.ds(h * width, width)], q_buf.at[h], q_sem.at[h]
        )
        for h in range(kv_heads)
    ]

    gain_copies = [
        pltpu.make_async_copy(src, gains.at[i], gain_sem.at[i])
        for i, src in enumerate((qg_hbm, kg_hbm))
    ]

    def remote(d, h, i):
        src = (k_hbm, v_hbm)[i]
        return pltpu.make_async_remote_copy(
            src_ref=src.at[:, pl.ds(h * head, head)],
            dst_ref=kv_prev.at[d - 1, i, h],
            send_sem=send_sem.at[d - 1, i, h],
            recv_sem=recv_sem.at[d - 1, i, h],
            device_id=device_of(stretch + d),
            device_id_type=MESH,
        )

    for copy in gain_copies + own_copies[:1] + q_copies + own_copies[1:]:
        copy.start()

    for d in range(1, span + 1):

        @pl.when(stretch + d <= last)
        def _():
            pl.semaphore_wait(barrier, 1)

    for h in range(kv_heads):
        for i in range(2):
            for d in range(1, span + 1):

                @pl.when(stretch + d <= last)
                def _(d=d, h=h, i=i):
                    remote(d, h, i).start()

    for d in range(1, span + 1):

        @pl.when(stretch < d)
        def _(d=d):
            kv_prev[d - 1] = jnp.zeros_like(kv_prev[d - 1])

    half = head // 2
    lane = lax.broadcasted_iota(jnp.int32, (1, head), 1)
    frequency = jnp.exp(
        lax.rem(lane, half).astype(jnp.float32) * (-2.0 * math.log(ROPE_BASE) / head)
    )
    sign = jnp.where(lane < half, -1.0, 1.0)
    for copy in gain_copies:
        copy.wait()
    q_gain, k_gain = gains[0], gains[1]
    q_swap, k_swap = pltpu.roll(q_gain, half, 1), pltpu.roll(k_gain, half, 1)
    tables = functools.partial(rope_tables, rows=rows, frequency=frequency, sign=sign)
    tab[0, 0], tab[0, 1] = tables(stretch * rows, gain=q_gain, gain_swapped=q_swap)
    for d in range(span + 1):
        tab[d + 1, 0], tab[d + 1, 1] = tables(
            (stretch - d) * rows, gain=k_gain, gain_swapped=k_swap
        )

    own_copies[0].wait()
    for h in range(kv_heads):
        k_cat[h, :rows] = rotate(
            kv_own[0, :, h * head : (h + 1) * head], tab[1, 0], tab[1, 1]
        )
    for h in range(kv_heads):
        q_copies[h].wait()
        for g in range(group):
            q_rot[h, g * rows : (g + 1) * rows] = rotate(
                q_buf[h, :, g * head : (g + 1) * head], tab[0, 0], tab[0, 1]
            )
    own_copies[1].wait()
    for h in range(kv_heads):
        v_cat[h, :rows] = kv_own[1, :, h * head : (h + 1) * head]

    row = lax.broadcasted_iota(jnp.int32, (rows, rows), 0)
    col = lax.broadcasted_iota(jnp.int32, (rows, rows), 1)
    own = col <= row
    scale = 1.0 / math.sqrt(head)
    bias = [
        jnp.where(stretch >= d, 0.0, NEG_FILL).astype(jnp.float32)
        for d in range(1, span + 1)
    ]

    for h in range(kv_heads):
        for d in range(1, span + 1):

            @pl.when(stretch >= d)
            def _(d=d, h=h):
                remote(d, h, 0).wait_recv()

            k_cat[h, d * rows : (d + 1) * rows] = rotate(
                kv_prev[d - 1, 0, h], tab[d + 1, 0], tab[d + 1, 1]
            )

            @pl.when(stretch >= d)
            def _(d=d, h=h):
                remote(d, h, 1).wait_recv()

            v_cat[h, d * rows : (d + 1) * rows] = kv_prev[d - 1, 1, h]

        keys, values = k_cat[h], v_cat[h]
        for g in range(group):
            scores = lax.dot_general(
                q_rot[h, g * rows : (g + 1) * rows],
                keys,
                (((1,), (1,)), ((), ())),
                preferred_element_type=jnp.float32,
            )
            parts = [scores[:, d * rows : (d + 1) * rows] for d in range(span + 1)]
            tiles = [jnp.where(own, parts[0], parts[span] + bias[span - 1])]
            tiles += [parts[d] + bias[d - 1] for d in range(1, span)]
            top = functools.reduce(jnp.maximum, tiles)
            top = jnp.max(top, axis=-1, keepdims=True)
            weights = [jnp.exp((tile - top) * scale) for tile in tiles]
            total = jnp.sum(functools.reduce(jnp.add, weights), axis=-1, keepdims=True)
            near = jnp.where(own, weights[0], 0.0)
            far = jnp.where(own, 0.0, weights[0])
            rounded = jnp.concatenate([near] + weights[1:] + [far], axis=1)
            mixed = jnp.dot(
                rounded.astype(jnp.bfloat16), values, preferred_element_type=jnp.float32
            )
            o_ref[:, h * width + g * head : h * width + (g + 1) * head] = (
                mixed / total
            ).astype(o_ref.dtype)

    for h in range(kv_heads):
        for i in range(2):
            for d in range(1, span + 1):

                @pl.when(stretch + d <= last)
                def _(d=d, h=h, i=i):
                    remote(d, h, i).wait_send()


def in_hbm(array):
    return pltpu.with_memory_space_constraint(array, pltpu.HBM)


def local(query_proj, key_proj, value_projection, query_gain, key_gain):
    cycle = lax.axis_size("blk")
    span = max(1, cycle // 64)
    rows, head = query_proj.shape[0], query_gain.shape[0]
    kv_heads = key_proj.shape[1] // head
    group = query_proj.shape[1] // head // kv_heads
    bf16 = jnp.bfloat16
    vmem = pl.BlockSpec(memory_space=pltpu.VMEM)
    hbm = pl.BlockSpec(memory_space=pltpu.HBM)
    return pl.pallas_call(
        functools.partial(kernel, cycle, span, kv_heads, group),
        out_shape=jax.ShapeDtypeStruct(query_proj.shape, bf16),
        in_specs=[hbm] * 5,
        out_specs=vmem,
        scratch_shapes=[
            pltpu.VMEM((kv_heads, rows, group * head), bf16),
            pltpu.VMEM((2, rows, kv_heads * head), bf16),
            pltpu.VMEM((span, 2, kv_heads, rows, head), bf16),
            pltpu.VMEM((kv_heads, group * rows, head), bf16),
            pltpu.VMEM((kv_heads, (span + 1) * rows, head), bf16),
            pltpu.VMEM((kv_heads, (span + 1) * rows, head), bf16),
            pltpu.VMEM((span + 2, 2, rows, head), jnp.float32),
            pltpu.VMEM((2, 1, head), jnp.float32),
            pltpu.SemaphoreType.DMA((kv_heads,)),
            pltpu.SemaphoreType.DMA((2,)),
            pltpu.SemaphoreType.DMA((2,)),
            pltpu.SemaphoreType.DMA((span, 2, kv_heads)),
            pltpu.SemaphoreType.DMA((span, 2, kv_heads)),
        ],
        compiler_params=pltpu.CompilerParams(
            collective_id=0, has_side_effects=True, vmem_limit_bytes=16 * 1024 * 1024
        ),
        name="window_attention",
    )(
        in_hbm(query_proj),
        in_hbm(key_proj),
        in_hbm(value_projection),
        in_hbm(query_gain.reshape(1, head)),
        in_hbm(key_gain.reshape(1, head)),
    )


def solution(mesh):
    rows = P(("groups", "blk", "uly"), None)
    return jax.shard_map(
        local,
        mesh=mesh,
        in_specs=(rows, rows, rows, P(), P()),
        out_specs=rows,
        check_vma=False,
    )
```
